32 devices in a mesh: src: 4 (over y, x), cell: 8 (over z, core).
Axes of the slice: x: 2, y: 2, z: 4, core: 2. Of those that a mesh axis runs over, the one named last changes fastest.
Arguments:
- green_source: bfloat16 [32, 8192], P('src', 'cell'), may hold values from -6 to 6
- green_receiver: bfloat16 [64, 8192], P('src', 'cell'), may hold values from -6 to 6
- pair_source: int32 [2048], P('src'), may hold values from 0 to 7
- pair_receiver: int32 [2048], P('src'), may hold values from 0 to 63
- cell_order: int32 [8, 1024], P('cell'), may hold values from 0 to 1023, each once within a row
- test_models: bfloat16 [128, 8192], P(None, 'cell'), may hold values from -6 to 6
- data_noise: bfloat16 [2048, 128], P('src'), may hold values from -8 to 8
Outputs:
- recovered: float32 [128, 8192], P('src', 'cell')
- data_residual: float32 [2048, 128], P(('src', 'cell'))
The draws below stay inside these ranges and needn't reach their ends.
Inputs may be any that keep to these rules, and one draw needn't show every extreme that they name: Each row of cell_order holds every number of 0 to 1023 once.
All inputs are finite; a program needn't handle non-finite values.
Results may differ from the reference program's by a relative error of at most 0.012.
Values may be sent and summed in bfloat16 or wider, within the bound.
A program may use at most 64 MiB of HBM per device.

```python
import math
import jax
import jax.numpy as jnp
from jax import lax

S_DEV = 8
R = 64
CD = 1024
NM = 128
HSTEPS = 2
PD = 512
PAIRS = 2048
TILES = 8
CELLS = 8192
SOURCES = 32


def place_ends(values, rng, smallest, top_value):
    longest = values.shape.index(max(values.shape))
    spots = []
    for shift in (0, 1):
        where = [jax.random.randint(jax.random.fold_in(rng, axis), (), 0, length) for axis, length in enumerate(values.shape)]
        where[longest] = (where[longest] + shift) % values.shape[longest]
        spots.append(tuple(where))
    return values.at[spots[0]].set(smallest).at[spots[1]].set(top_value)


def block_levels(rng, dims, shards, low, high):
    factor_of = 1.0
    for position, blocks in shards:
        draws = jax.random.uniform(jax.random.fold_in(jax.random.fold_in(rng, 6), position), (blocks,), jnp.float32, low / len(shards), high / len(shards))
        factor_of = factor_of * jnp.repeat(jnp.exp(draws), dims[position] // blocks).reshape((-1,) + (1,) * (len(dims) - 1 - position))
    return factor_of


def noise(rng, shape, scale, most, cuts=(), kind=jnp.bfloat16):
    drawn = scale * jax.random.normal(rng, shape, jnp.float32)
    if cuts:
        drawn = drawn * block_levels(rng, shape, cuts, -0.22, 0.18)
    return jnp.clip(drawn, -most, most).astype(kind)


def setup_inputs(seed: int = 0) -> dict:
    key_of = jax.random.split(jax.random.key(seed), 8)
    green_source = noise(key_of[0], (SOURCES, CELLS), 1.0, 6.0, ((0, 4), (1, 8)))
    green_receiver = noise(key_of[1], (R, CELLS), 1.0, 6.0, ((0, 4), (1, 8)))
    pair_source = place_ends(jax.random.randint(key_of[2], (PAIRS,), 0, S_DEV), jax.random.fold_in(key_of[2], 1), 0, S_DEV - 1).astype(jnp.int32)
    pair_receiver = place_ends(jax.random.randint(key_of[3], (PAIRS,), 0, R), jax.random.fold_in(key_of[3], 1), 0, R - 1).astype(jnp.int32)
    cell_order = jax.vmap(lambda own: jax.random.permutation(own, CD))(jax.random.split(key_of[4], TILES)).reshape((TILES, CD)).astype(jnp.int32)
    test_models = noise(key_of[5], (NM, CELLS), 1.0, 6.0, ((1, 8),))
    data_noise = noise(key_of[6], (PAIRS, NM), 0.5, 8.0, ((0, 4),))
    return dict(green_source=green_source, green_receiver=green_receiver, pair_source=pair_source, pair_receiver=pair_receiver, cell_order=cell_order, test_models=test_models, data_noise=data_noise)


def reference(green_source, green_receiver, pair_source, pair_receiver, cell_order, test_models, data_noise):
    scale = 1.0 / math.sqrt(CELLS)
    columns = (jnp.arange(TILES, dtype=jnp.int32)[:, None] * CD + cell_order).reshape(-1).astype(jnp.int32)
    source_tiles = jnp.take(green_source, columns, axis=1).reshape(SOURCES, TILES, CD).transpose(1, 0, 2)
    receiver_tiles = jnp.take(green_receiver, columns, axis=1).reshape(R, TILES, CD).transpose(1, 0, 2)
    source_rows = (jnp.arange(PAIRS, dtype=jnp.int32) // PD * S_DEV + pair_source).astype(jnp.int32)

    def tile_kernel(tile):
        left = jnp.take(source_tiles[tile], source_rows, axis=0).astype(jnp.float32)
        right = jnp.take(receiver_tiles[tile], pair_receiver, axis=0).astype(jnp.float32)
        rounded = lax.optimization_barrier((left * right).astype(jnp.bfloat16))
        return rounded.astype(jnp.float32)

    def forward(models):
        model_tiles = models.reshape(NM, TILES, CD).transpose(1, 0, 2)

        def add_tile(total, tile):
            kernel = tile_kernel(tile)
            return (total + jnp.dot(kernel, model_tiles[tile].T, precision=lax.Precision.HIGHEST), None)
        total, unused = lax.scan(add_tile, jnp.zeros((PAIRS, NM), jnp.float32), jnp.arange(TILES, dtype=jnp.int32))
        return total * scale

    def adjoint(weighted):

        def one_tile(tile):
            return jnp.dot(weighted.T, tile_kernel(tile), precision=lax.Precision.HIGHEST)
        parts = lax.map(one_tile, jnp.arange(TILES, dtype=jnp.int32))
        return parts.transpose(1, 0, 2).reshape(NM, CELLS) * scale
    observed = forward(test_models.astype(jnp.float32)) + data_noise.astype(jnp.float32)
    residual = -observed
    recovered = jnp.zeros((NM, CELLS), jnp.float32)
    for step in range(HSTEPS):
        spread = lax.optimization_barrier(jnp.sum(residual * residual, axis=0))
        delta = 1.0 * jnp.sqrt(spread / PAIRS + 1e-06)
        weight = delta[None, :] / jnp.maximum(jnp.abs(residual), delta[None, :])
        weighted = lax.optimization_barrier((weight * residual).astype(jnp.bfloat16)).astype(jnp.float32)
        grad = adjoint(weighted)
        grad_low = lax.optimization_barrier(grad.astype(jnp.bfloat16)).astype(jnp.float32)
        image = forward(grad_low)
        curvature = lax.optimization_barrier(jnp.sum(weight * image * image, axis=0))
        numer = lax.optimization_barrier(jnp.sum(grad * grad, axis=1))
        alpha = numer / (curvature + 1e-06)
        recovered = recovered - alpha[:, None] * grad
        residual = residual - alpha[None, :] * image
    return (recovered, residual)
```

```python
import functools
import math

import jax
import jax.numpy as jnp
from jax import lax
from jax.experimental import pallas as pl
from jax.experimental.pallas import tpu as pltpu
from jax.sharding import PartitionSpec as P

HSTEPS = 2
MESH = pl.DeviceIdType.MESH
F32 = jnp.float32
BF16 = jnp.bfloat16
NT = (((1,), (1,)), ((), ()))


def each(count, body, start=0):
    if count - start <= 8:
        for i in range(start, count):
            body(i)
    else:

        def step(i, carry):
            body(i)
            return carry

        lax.fori_loop(start, count, step, 0)


def kernel_body(
    n_s, n_c,
    gs, gr, ps, pr, order, models, noise,
    rec_out, res_out,
    gs_all, gr_all, ps_all, pr_all, nz_send, nz_recv,
    oper, rs_send, rs_recv, ag, stat_send, stat_recv,
    fin_send, fin_recv, wlow, res, grads,
    in_send, in_recv, rs_ssem, rs_rsem, ag_ssem, ag_rsem, st_ssem, st_rsem, fin_ssem, fin_rsem,
):
    s = lax.axis_index("src")
    c = lax.axis_index("cell")
    group_pairs = ps.shape[1]
    cells = gs.shape[1]
    models_count = models.shape[0]
    own = models_count // n_s
    share = group_pairs // n_c
    chunk = share * n_s
    pairs_all = group_pairs * n_s
    s_dev = gs.shape[0]
    receivers = gr.shape[0] * n_s
    scale = 1.0 / math.sqrt(cells * n_c)

    def src_peer(j):
        return lax.rem(s + j, n_s)

    def src_from(j):
        return lax.rem(s + n_s - j, n_s)

    def cell_peer(j):
        return lax.rem(c + j, n_c)

    def cell_from(j):
        return lax.rem(c + n_c - j, n_c)

    def to_src(src_ref, dst_ref, ssem, rsem, peer):
        return pltpu.make_async_remote_copy(
            src_ref=src_ref, dst_ref=dst_ref, send_sem=ssem, recv_sem=rsem,
            device_id={"src": peer}, device_id_type=MESH,
        )

    def to_cell(src_ref, dst_ref, ssem, rsem, peer):
        return pltpu.make_async_remote_copy(
            src_ref=src_ref, dst_ref=dst_ref, send_sem=ssem, recv_sem=rsem,
            device_id={"cell": peer}, device_id_type=MESH,
        )

    barrier = pltpu.get_barrier_semaphore()
    each(n_s, lambda j: pl.semaphore_signal(
        barrier, inc=1, device_id={"src": src_peer(j)}, device_id_type=MESH), 1)
    each(n_c, lambda j: pl.semaphore_signal(
        barrier, inc=1, device_id={"cell": cell_peer(j)}, device_id_type=MESH), 1)

    nz = noise[pl.ds(pl.multiple_of(c * share, share), share), :].astype(F32)
    nz_send[...] = nz.T.reshape(n_s, own, share).astype(BF16)

    pl.semaphore_wait(barrier, n_s + n_c - 2)

    def in_copies(j, slot, peer):
        return [
            to_src(gs, gs_all.at[slot], in_send.at[0, j], in_recv.at[0, j], peer),
            to_src(gr, gr_all.at[slot], in_send.at[1, j], in_recv.at[1, j], peer),
            to_src(ps, ps_all.at[slot], in_send.at[2, j], in_recv.at[2, j], peer),
            to_src(pr, pr_all.at[slot], in_send.at[3, j], in_recv.at[3, j], peer),
            to_src(nz_send.at[peer], nz_recv.at[slot], in_send.at[4, j], in_recv.at[4, j], peer),
        ]

    def start_inputs(j):
        for copy in in_copies(j, s, src_peer(j)):
            copy.start()

    each(n_s, start_inputs, 1)
    gs_all[s] = gs[...]
    gr_all[s] = gr[...]
    ps_all[s] = ps[...]
    pr_all[s] = pr[...]
    nz_recv[s] = nz_send[s]

    rows = lax.broadcasted_iota(jnp.int32, (cells, cells), 0)
    select = jnp.where(rows == order[...], 1.0, 0.0).astype(BF16)

    def wait_inputs(j):
        for copy in in_copies(j, src_from(j), src_peer(j)):
            copy.wait_recv()

    each(n_s, wait_inputs, 1)

    sources = n_s * s_dev
    fields = jnp.concatenate(
        [
            gs_all[...].astype(F32).reshape(sources, cells),
            gr_all[...].astype(F32).reshape(receivers, cells),
        ],
        axis=0,
    ).astype(BF16)
    placed = jnp.dot(fields, select, preferred_element_type=F32)
    source_cols = placed[:sources].astype(BF16)
    receiver_cols = placed[sources:].astype(BF16)

    def build(k):
        source_rows = lax.broadcasted_iota(jnp.int32, (sources, group_pairs), 0)
        receiver_rows = lax.broadcasted_iota(jnp.int32, (receivers, group_pairs), 0)
        pick_s = jnp.where(source_rows == ps_all[k] + k * s_dev, 1.0, 0.0).T.astype(BF16)
        pick_r = jnp.where(receiver_rows == pr_all[k], 1.0, 0.0).T.astype(BF16)
        block = (
            jnp.dot(pick_s, source_cols, preferred_element_type=F32)
            * jnp.dot(pick_r, receiver_cols, preferred_element_type=F32)
        ).astype(BF16)
        for t in range(n_c):
            at = pl.multiple_of(t * chunk + k * share, share)
            oper[pl.ds(at, share), :] = block[t * share : (t + 1) * share]

    def build_step(k, carry):
        build(k)
        return carry

    lax.fori_loop(0, n_s, build_step, 0)

    def rs_copy(phase, j, target):
        return to_cell(
            rs_send.at[phase, target], rs_recv.at[phase, j],
            rs_ssem.at[phase, j], rs_rsem.at[phase, j], target,
        )

    def forward(phase, low):
        def part(k):
            at = pl.multiple_of(k * chunk, chunk)
            return lax.dot_general(low, oper[pl.ds(at, chunk), :], NT, preferred_element_type=F32)

        def one(j):
            target = cell_peer(j)
            rs_send[phase, target] = part(target).astype(BF16)
            rs_copy(phase, j, target).start()

        each(n_c, one, 1)
        rs_total = part(c)
        each(n_c, lambda j: rs_copy(phase, j, cell_peer(j)).wait_recv(), 1)
        for j in range(1, n_c):
            rs_total = rs_total + rs_recv[phase, j].astype(F32)
        return rs_total * scale

    def ag_copy(phase, j, slot):
        return to_cell(
            ag.at[phase, slot], ag.at[phase, slot],
            ag_ssem.at[phase, j], ag_rsem.at[phase, j], cell_peer(j),
        )

    def gather(phase, value):
        ag[phase, c] = value.astype(BF16)
        each(n_c, lambda j: ag_copy(phase, j, c).start(), 1)
        each(n_c, lambda j: ag_copy(phase, j, cell_from(j)).wait_recv(), 1)
        return ag[phase].astype(F32)

    def stat_copy(step, j):
        return to_cell(
            stat_send.at[step], stat_recv.at[step, j],
            st_ssem.at[step, j], st_rsem.at[step, j], cell_peer(j),
        )

    def stat_start(step, columns):
        stacked = jnp.concatenate(
            [jnp.broadcast_to(column, (own, 128 // len(columns))) for column in columns], axis=1
        )
        stat_send[step] = stacked
        each(n_c, lambda j: stat_copy(step, j).start(), 1)

    def stat_total(step):
        each(n_c, lambda j: stat_copy(step, j).wait_recv(), 1)
        total = stat_send[step]
        for j in range(1, n_c):
            total = total + stat_recv[step, j]
        return total

    own_models = models[pl.ds(pl.multiple_of(s * own, own), own), :]
    own_noise = jnp.concatenate([nz_recv[k].astype(F32) for k in range(n_s)], axis=1)
    chunk_res = -(forward(0, own_models) + own_noise)
    res[...] = gather(0, chunk_res)

    def pair_sum(values):
        return jnp.sum(jnp.sum(values, axis=0), axis=1, keepdims=True)

    for step in range(HSTEPS):
        last = step == HSTEPS - 1
        full = res[...]
        spread = pair_sum(full * full)
        delta = jnp.sqrt(spread / pairs_all + 1e-06)
        weight = delta[None] / jnp.maximum(jnp.abs(full), delta[None])
        weighted = weight * full
        for k in range(n_c):
            wlow[:, k * chunk : (k + 1) * chunk] = weighted[k].astype(BF16)
        grad = jnp.dot(wlow[...], oper[...], preferred_element_type=F32) * scale
        grads[step] = grad
        numer_own = jnp.sum(grad * grad, axis=1, keepdims=True)
        if not last:
            stat_start(step, [numer_own])
        image = forward(step + 1, grad.astype(BF16))
        if last:
            own_full = chunk_res
            own_weight = delta / jnp.maximum(jnp.abs(own_full), delta)
            curve_own = jnp.sum(own_weight * image * image, axis=1, keepdims=True)
            stat_start(step, [numer_own, curve_own])
            total = stat_total(step)
            numer = total[:, 0:1]
            curvature = total[:, 64:65]
            alpha = numer / (curvature + 1e-06)
        else:
            images = gather(step + 1, image)
            numer = stat_total(step)[:, 0:1]
            curvature = pair_sum(weight * images * images)
            alpha = numer / (curvature + 1e-06)
            res[...] = full - alpha[None] * images
            grads[step] = alpha * grads[step]
        chunk_res = chunk_res - alpha * image

    for k in range(n_s):
        fin_send[k] = chunk_res[:, k * share : (k + 1) * share]

    def fin_copy(j, slot):
        return to_src(
            fin_send.at[src_peer(j)], fin_recv.at[slot], fin_ssem.at[j], fin_rsem.at[j], src_peer(j)
        )

    each(n_s, lambda j: fin_copy(j, s).start(), 1)
    fin_recv[s] = fin_send[s]
    total_rec = -(alpha * grads[HSTEPS - 1])
    for step in range(HSTEPS - 1):
        total_rec = total_rec - grads[step]
    rec_out[...] = total_rec

    def in_done(j):
        for copy in in_copies(j, s, src_peer(j)):
            copy.wait_send()

    each(n_s, in_done, 1)
    for phase in range(HSTEPS + 1):
        each(n_c, lambda j, phase=phase: rs_copy(phase, j, cell_peer(j)).wait_send(), 1)
    for phase in range(HSTEPS):
        each(n_c, lambda j, phase=phase: ag_copy(phase, j, c).wait_send(), 1)
        each(n_c, lambda j, phase=phase: stat_copy(phase, j).wait_send(), 1)
    each(n_s, lambda j: fin_copy(j, src_from(j)).wait_recv(), 1)
    res_out[...] = fin_recv[...].reshape(models_count, share).T
    each(n_s, lambda j: fin_copy(j, s).wait_send(), 1)


def shards(
    green_source, green_receiver, pair_source, pair_receiver, cell_order, test_models, data_noise
):
    n_s = lax.axis_size("src")
    n_c = lax.axis_size("cell")
    s_dev, cells = green_source.shape
    r_dev = green_receiver.shape[0]
    group_pairs = pair_source.shape[0]
    models_count = test_models.shape[0]
    own = models_count // n_s
    share = group_pairs // n_c
    chunk = share * n_s
    pairs_all = group_pairs * n_s
    dma = pltpu.SemaphoreType.DMA
    return pl.pallas_call(
        functools.partial(kernel_body, n_s, n_c),
        out_shape=(
            jax.ShapeDtypeStruct((own, cells), F32),
            jax.ShapeDtypeStruct((share, models_count), F32),
        ),
        in_specs=[pl.BlockSpec(memory_space=pltpu.VMEM)] * 7,
        out_specs=[pl.BlockSpec(memory_space=pltpu.VMEM)] * 2,
        scratch_shapes=[
            pltpu.VMEM((n_s, s_dev, cells), BF16),
            pltpu.VMEM((n_s, r_dev, cells), BF16),
            pltpu.VMEM((n_s, 1, group_pairs), jnp.int32),
            pltpu.VMEM((n_s, 1, group_pairs), jnp.int32),
            pltpu.VMEM((n_s, own, share), BF16),
            pltpu.VMEM((n_s, own, share), BF16),
            pltpu.VMEM((pairs_all, cells), BF16),
            pltpu.VMEM((HSTEPS + 1, n_c, own, chunk), BF16),
            pltpu.VMEM((HSTEPS + 1, n_c, own, chunk), BF16),
            pltpu.VMEM((HSTEPS, n_c, own, chunk), BF16),
            pltpu.VMEM((HSTEPS, own, 128), F32),
            pltpu.VMEM((HSTEPS, n_c, own, 128), F32),
            pltpu.VMEM((n_s, own, share), F32),
            pltpu.VMEM((n_s, own, share), F32),
            pltpu.VMEM((own, pairs_all), BF16),
            pltpu.VMEM((n_c, own, chunk), F32),
            pltpu.VMEM((HSTEPS, own, cells), F32),
            dma((5, n_s)), dma((5, n_s)),
            dma((HSTEPS + 1, n_c)), dma((HSTEPS + 1, n_c)),
            dma((HSTEPS, n_c)), dma((HSTEPS, n_c)),
            dma((HSTEPS, n_c)), dma((HSTEPS, n_c)),
            dma((n_s,)), dma((n_s,)),
        ],
        compiler_params=pltpu.CompilerParams(
            collective_id=0, has_side_effects=True, vmem_limit_bytes=56 * 1024 * 1024
        ),
    )(
        green_source, green_receiver, pair_source[None, :], pair_receiver[None, :],
        cell_order, test_models, data_noise,
    )


def solution(mesh):
    return jax.shard_map(
        shards,
        mesh=mesh,
        in_specs=(
            P("src", "cell"),
            P("src", "cell"),
            P("src"),
            P("src"),
            P("cell", None),
            P(None, "cell"),
            P("src", None),
        ),
        out_specs=(P("src", "cell"), P(("src", "cell"), None)),
        check_vma=False,
    )
```

```python
import functools
import math

import jax
import jax.numpy as jnp
from jax import lax
from jax.experimental import pallas as pl
from jax.experimental.pallas import tpu as pltpu
from jax.sharding import PartitionSpec as P

HSTEPS = 2
MESH = pl.DeviceIdType.MESH
F32 = jnp.float32
BF16 = jnp.bfloat16
NT = (((1,), (1,)), ((), ()))


def each(count, body):
    if count <= 8:
        for i in range(count - 1, 0, -1):
            body(i)
    else:

        def step(i, carry):
            body(count - i)
            return carry

        lax.fori_loop(1, count, step, 0)


def kernel_body(
    n_s, n_c,
    gs, gr, ps, pr, order, models, noise,
    rec_out, res_out,
    gs_in, gr_in, order_in, models_in, noise_in,
    fields, indices, nz_send, nz_recv,
    oper, rs_send, rs_recv, ag, stat_send, stat_recv,
    fin_send, fin_recv, wlow, res, grads,
    load, in_send, in_recv, rs_ssem, rs_rsem, ag_ssem, ag_rsem, st_ssem, st_rsem, fin_ssem, fin_rsem,
):
    s = lax.axis_index("src")
    c = lax.axis_index("cell")
    group_pairs = ps.shape[1]
    cells = gs.shape[1]
    models_count = models.shape[0]
    own = models_count // n_s
    share = group_pairs // n_c
    chunk = share * n_s
    pairs_all = group_pairs * n_s
    s_dev = gs.shape[0]
    receivers = gr.shape[0] * n_s
    scale = 1.0 / math.sqrt(cells * n_c)

    def src_peer(j):
        return jnp.bitwise_xor(s, j)

    def cell_peer(j):
        return jnp.bitwise_xor(c, j)

    def to_src(src_ref, dst_ref, ssem, rsem, peer):
        return pltpu.make_async_remote_copy(
            src_ref=src_ref, dst_ref=dst_ref, send_sem=ssem, recv_sem=rsem,
            device_id={"src": peer}, device_id_type=MESH,
        )

    def to_cell(src_ref, dst_ref, ssem, rsem, peer):
        return pltpu.make_async_remote_copy(
            src_ref=src_ref, dst_ref=dst_ref, send_sem=ssem, recv_sem=rsem,
            device_id={"cell": peer}, device_id_type=MESH,
        )

    barrier = pltpu.get_barrier_semaphore()
    each(n_s, lambda j: pl.semaphore_signal(
        barrier, inc=1, device_id={"src": src_peer(j)}, device_id_type=MESH))
    each(n_c, lambda j: pl.semaphore_signal(
        barrier, inc=1, device_id={"cell": cell_peer(j)}, device_id_type=MESH))

    loads = [
        pltpu.make_async_copy(order, order_in, load.at[0]),
        pltpu.make_async_copy(gs, gs_in, load.at[1]),
        pltpu.make_async_copy(gr, gr_in, load.at[2]),
        pltpu.make_async_copy(ps, indices.at[s, 0], load.at[3]),
        pltpu.make_async_copy(pr, indices.at[s, 1], load.at[4]),
        pltpu.make_async_copy(
            noise.at[pl.ds(pl.multiple_of(c * share, share), share), :], noise_in, load.at[5]),
        pltpu.make_async_copy(
            models.at[pl.ds(pl.multiple_of(s * own, own), own), :], models_in, load.at[6]),
    ]
    for copy in loads:
        copy.start()
    for copy in loads:
        copy.wait()
    rows = lax.broadcasted_iota(jnp.int32, (cells, cells), 0)
    select = jnp.where(rows == order_in[...], 1.0, 0.0).astype(BF16)
    raw = jnp.concatenate([gs_in[...].astype(F32), gr_in[...].astype(F32)], axis=0).astype(BF16)
    fields[s] = jnp.dot(raw, select, preferred_element_type=F32).astype(BF16)
    nz_send[...] = noise_in[...].astype(F32).T.reshape(n_s, own, share).astype(BF16)
    nz_recv[s] = nz_send[s]

    pl.semaphore_wait(barrier, n_s + n_c - 2)

    def in_copies(j, slot):
        peer = src_peer(j)
        return [
            to_src(fields.at[slot], fields.at[slot], in_send.at[0, j], in_recv.at[0, j], peer),
            to_src(indices.at[slot], indices.at[slot], in_send.at[1, j], in_recv.at[1, j], peer),
            to_src(nz_send.at[peer], nz_recv.at[slot], in_send.at[2, j], in_recv.at[2, j], peer),
        ]

    def start_inputs(j):
        for copy in in_copies(j, s):
            copy.start()

    each(n_s, start_inputs)

    def wait_inputs(j):
        for copy in in_copies(j, src_peer(j)):
            copy.wait_recv()

    each(n_s, wait_inputs)

    sources = n_s * s_dev
    every = fields[...].astype(F32)
    source_cols = every[:, :s_dev].reshape(sources, cells).astype(BF16)
    receiver_cols = every[:, s_dev:].reshape(receivers, cells).astype(BF16)

    def build(k):
        source_rows = lax.broadcasted_iota(jnp.int32, (sources, group_pairs), 0)
        receiver_rows = lax.broadcasted_iota(jnp.int32, (receivers, group_pairs), 0)
        pick_s = jnp.where(source_rows == indices[k, 0] + k * s_dev, 1.0, 0.0).T.astype(BF16)
        pick_r = jnp.where(receiver_rows == indices[k, 1], 1.0, 0.0).T.astype(BF16)
        block = (
            jnp.dot(pick_s, source_cols, preferred_element_type=F32)
            * jnp.dot(pick_r, receiver_cols, preferred_element_type=F32)
        ).astype(BF16)
        for t in range(n_c):
            at = pl.multiple_of(t * chunk + k * share, share)
            oper[pl.ds(at, share), :] = block[t * share : (t + 1) * share]

    def build_step(k, carry):
        build(k)
        return carry

    lax.fori_loop(0, n_s, build_step, 0)

    def rs_copy(phase, j, target):
        return to_cell(
            rs_send.at[phase, target], rs_recv.at[phase, j],
            rs_ssem.at[phase, j], rs_rsem.at[phase, j], target,
        )

    def forward(phase, low):
        def part(k):
            at = pl.multiple_of(k * chunk, chunk)
            return lax.dot_general(low, oper[pl.ds(at, chunk), :], NT, preferred_element_type=F32)

        def one(j):
            target = cell_peer(j)
            rs_send[phase, target] = part(target).astype(BF16)
            rs_copy(phase, j, target).start()

        each(n_c, one)
        rs_total = part(c)
        each(n_c, lambda j: rs_copy(phase, j, cell_peer(j)).wait_recv())
        for j in range(1, n_c):
            rs_total = rs_total + rs_recv[phase, j].astype(F32)
        return rs_total * scale

    def ag_copy(phase, j, slot):
        return to_cell(
            ag.at[phase, slot], ag.at[phase, slot],
            ag_ssem.at[phase, j], ag_rsem.at[phase, j], cell_peer(j),
        )

    def gather(phase, value):
        ag[phase, c] = value.astype(BF16)
        each(n_c, lambda j: ag_copy(phase, j, c).start())
        each(n_c, lambda j: ag_copy(phase, j, cell_peer(j)).wait_recv())
        return ag[phase].astype(F32)

    def stat_copy(step, j):
        return to_cell(
            stat_send.at[step], stat_recv.at[step, j],
            st_ssem.at[step, j], st_rsem.at[step, j], cell_peer(j),
        )

    diagonal = lax.broadcasted_iota(jnp.int32, (own, own), 0) == lax.broadcasted_iota(
        jnp.int32, (own, own), 1
    )

    def to_row(column):
        return jnp.sum(jnp.where(diagonal, column, 0.0), axis=0, keepdims=True)

    def to_column(row):
        return jnp.sum(jnp.where(diagonal, row, 0.0), axis=1, keepdims=True)

    def stat_start(step, first, second):
        top = lax.broadcasted_iota(jnp.int32, (8, own), 0) == 0
        stat_send[step] = jnp.where(top, to_row(first), to_row(second))
        each(n_c, lambda j: stat_copy(step, j).start())

    def stat_total(step):
        each(n_c, lambda j: stat_copy(step, j).wait_recv())
        total = stat_send[step]
        for j in range(1, n_c):
            total = total + stat_recv[step, j]
        return to_column(total[0:1]), to_column(total[1:2])

    own_models = models_in[...]
    own_noise = jnp.concatenate([nz_recv[k].astype(F32) for k in range(n_s)], axis=1)
    chunk_res = -(forward(0, own_models) + own_noise)
    res[...] = gather(0, chunk_res)

    def pair_sum(values):
        return jnp.sum(jnp.sum(values, axis=0), axis=1, keepdims=True)

    for step in range(HSTEPS):
        last = step == HSTEPS - 1
        full = res[...]
        spread = pair_sum(full * full)
        delta = jnp.sqrt(spread / pairs_all + 1e-06)
        weight = delta[None] / jnp.maximum(jnp.abs(full), delta[None])
        weighted = weight * full
        for k in range(n_c):
            wlow[:, k * chunk : (k + 1) * chunk] = weighted[k].astype(BF16)
        grad = jnp.dot(wlow[...], oper[...], preferred_element_type=F32) * scale
        grads[step] = grad
        numer_own = jnp.sum(grad * grad, axis=1, keepdims=True)
        if not last:
            stat_start(step, numer_own, numer_own)
        image = forward(step + 1, grad.astype(BF16))
        if last:
            own_full = chunk_res
            own_weight = delta / jnp.maximum(jnp.abs(own_full), delta)
            curve_own = jnp.sum(own_weight * image * image, axis=1, keepdims=True)
            stat_start(step, numer_own, curve_own)
            numer, curvature = stat_total(step)
            alpha = numer / (curvature + 1e-06)
        else:
            images = gather(step + 1, image)
            numer, _ = stat_total(step)
            curvature = pair_sum(weight * images * images)
            alpha = numer / (curvature + 1e-06)
            res[...] = full - alpha[None] * images
            grads[step] = alpha * grads[step]
        chunk_res = chunk_res - alpha * image

    for k in range(n_s):
        fin_send[k] = chunk_res[:, k * share : (k + 1) * share]

    def fin_copy(j, slot):
        return to_src(
            fin_send.at[src_peer(j)], fin_recv.at[slot], fin_ssem.at[j], fin_rsem.at[j], src_peer(j)
        )

    each(n_s, lambda j: fin_copy(j, s).start())
    fin_recv[s] = fin_send[s]
    total_rec = -(alpha * grads[HSTEPS - 1])
    for step in range(HSTEPS - 1):
        total_rec = total_rec - grads[step]
    rec_out[...] = total_rec

    def in_done(j):
        for copy in in_copies(j, s):
            copy.wait_send()

    each(n_s, in_done)
    for phase in range(HSTEPS + 1):
        each(n_c, lambda j, phase=phase: rs_copy(phase, j, cell_peer(j)).wait_send())
    for phase in range(HSTEPS):
        each(n_c, lambda j, phase=phase: ag_copy(phase, j, c).wait_send())
        each(n_c, lambda j, phase=phase: stat_copy(phase, j).wait_send())
    each(n_s, lambda j: fin_copy(j, src_peer(j)).wait_recv())
    res_out[...] = fin_recv[...].reshape(models_count, share).T
    each(n_s, lambda j: fin_copy(j, s).wait_send())


def shards(
    green_source, green_receiver, pair_source, pair_receiver, cell_order, test_models, data_noise
):
    n_s = lax.axis_size("src")
    n_c = lax.axis_size("cell")
    s_dev, cells = green_source.shape
    r_dev = green_receiver.shape[0]
    group_pairs = pair_source.shape[0]
    models_count = test_models.shape[0]
    own = models_count // n_s
    share = group_pairs // n_c
    chunk = share * n_s
    pairs_all = group_pairs * n_s
    dma = pltpu.SemaphoreType.DMA
    return pl.pallas_call(
        functools.partial(kernel_body, n_s, n_c),
        out_shape=(
            pltpu.VMEM((own, cells), F32),
            pltpu.VMEM((share, models_count), F32),
        ),
        in_specs=[pl.BlockSpec(memory_space=pltpu.HBM)] * 7,
        out_specs=[pl.BlockSpec(memory_space=pltpu.VMEM)] * 2,
        scratch_shapes=[
            pltpu.VMEM((s_dev, cells), BF16),
            pltpu.VMEM((r_dev, cells), BF16),
            pltpu.VMEM((1, cells), jnp.int32),
            pltpu.VMEM((own, cells), BF16),
            pltpu.VMEM((share, models_count), BF16),
            pltpu.VMEM((n_s, s_dev + r_dev, cells), BF16),
            pltpu.VMEM((n_s, 2, 1, group_pairs), jnp.int32),
            pltpu.VMEM((n_s, own, share), BF16),
            pltpu.VMEM((n_s, own, share), BF16),
            pltpu.VMEM((pairs_all, cells), BF16),
            pltpu.VMEM((HSTEPS + 1, n_c, own, chunk), BF16),
            pltpu.VMEM((HSTEPS + 1, n_c, own, chunk), BF16),
            pltpu.VMEM((HSTEPS, n_c, own, chunk), BF16),
            pltpu.VMEM((HSTEPS, 8, own), F32),
            pltpu.VMEM((HSTEPS, n_c, 8, own), F32),
            pltpu.VMEM((n_s, own, share), F32),
            pltpu.VMEM((n_s, own, share), F32),
            pltpu.VMEM((own, pairs_all), BF16),
            pltpu.VMEM((n_c, own, chunk), F32),
            pltpu.VMEM((HSTEPS, own, cells), F32),
            dma((7,)), dma((3, n_s)), dma((3, n_s)),
            dma((HSTEPS + 1, n_c)), dma((HSTEPS + 1, n_c)),
            dma((HSTEPS, n_c)), dma((HSTEPS, n_c)),
            dma((HSTEPS, n_c)), dma((HSTEPS, n_c)),
            dma((n_s,)), dma((n_s,)),
        ],
        compiler_params=pltpu.CompilerParams(
            collective_id=0, has_side_effects=True, vmem_limit_bytes=60 * 1024 * 1024
        ),
    )(
        green_source, green_receiver, pair_source[None, :], pair_receiver[None, :],
        cell_order, test_models, data_noise,
    )


def solution(mesh):
    return jax.shard_map(
        shards,
        mesh=mesh,
        in_specs=(
            P("src", "cell"),
            P("src", "cell"),
            P("src"),
            P("src"),
            P("cell", None),
            P(None, "cell"),
            P("src", None),
        ),
        out_specs=(P("src", "cell"), P(("src", "cell"), None)),
        check_vma=False,
    )
```

```python
import functools
import math

import jax
import jax.numpy as jnp
from jax import lax
from jax.experimental import pallas as pl
from jax.experimental.pallas import tpu as pltpu
from jax.sharding import PartitionSpec as P

HSTEPS = 2
MESH = pl.DeviceIdType.MESH
F32 = jnp.float32
BF16 = jnp.bfloat16
NT = (((1,), (1,)), ((), ()))


def each(count, body):
    if count <= 8:
        for i in range(count - 1, 0, -1):
            body(i)
    else:

        def step(i, carry):
            body(count - i)
            return carry

        lax.fori_loop(1, count, step, 0)


def kernel_body(
    n_s, n_c,
    gs, gr, ps, pr, order, models, noise,
    rec_out, res_out,
    gs_in, gr_in, order_in, models_in, noise_in,
    fields, indices, nz_send, nz_recv,
    picks, oper, rs_send, rs_recv, ag, stat_send, stat_recv,
    fin_send, fin_recv, wlow, res, grads,
    load, in_send, in_recv, rs_ssem, rs_rsem, ag_ssem, ag_rsem, st_ssem, st_rsem, fin_ssem, fin_rsem,
):
    s = lax.axis_index("src")
    c = lax.axis_index("cell")
    group_pairs = ps.shape[1]
    cells = gs.shape[1]
    models_count = models.shape[0]
    own = models_count // n_s
    share = group_pairs // n_c
    chunk = share * n_s
    pairs_all = group_pairs * n_s
    s_dev = gs.shape[0]
    r_dev = gr.shape[0]
    scale = 1.0 / math.sqrt(cells * n_c)

    def src_peer(j):
        return jnp.bitwise_xor(s, j)

    def cell_peer(j):
        return jnp.bitwise_xor(c, j)

    def to_src(src_ref, dst_ref, ssem, rsem, peer):
        return pltpu.make_async_remote_copy(
            src_ref=src_ref, dst_ref=dst_ref, send_sem=ssem, recv_sem=rsem,
            device_id={"src": peer}, device_id_type=MESH,
        )

    def to_cell(src_ref, dst_ref, ssem, rsem, peer):
        return pltpu.make_async_remote_copy(
            src_ref=src_ref, dst_ref=dst_ref, send_sem=ssem, recv_sem=rsem,
            device_id={"cell": peer}, device_id_type=MESH,
        )

    barrier = pltpu.get_barrier_semaphore()
    each(n_s, lambda j: pl.semaphore_signal(
        barrier, inc=1, device_id={"src": src_peer(j)}, device_id_type=MESH))
    each(n_c, lambda j: pl.semaphore_signal(
        barrier, inc=1, device_id={"cell": cell_peer(j)}, device_id_type=MESH))

    loads = [
        pltpu.make_async_copy(order, order_in, load.at[0]),
        pltpu.make_async_copy(gs, gs_in, load.at[1]),
        pltpu.make_async_copy(gr, gr_in, load.at[2]),
        pltpu.make_async_copy(ps, indices.at[s, 0], load.at[3]),
        pltpu.make_async_copy(pr, indices.at[s, 1], load.at[4]),
        pltpu.make_async_copy(
            noise.at[pl.ds(pl.multiple_of(c * share, share), share), :], noise_in, load.at[5]),
        pltpu.make_async_copy(
            models.at[pl.ds(pl.multiple_of(s * own, own), own), :], models_in, load.at[6]),
    ]
    for copy in loads:
        copy.start()
    for copy in loads:
        copy.wait()
    rows = lax.broadcasted_iota(jnp.int32, (cells, cells), 0)
    select = jnp.where(rows == order_in[...], 1.0, 0.0).astype(BF16)
    raw = jnp.concatenate([gs_in[...].astype(F32), gr_in[...].astype(F32)], axis=0).astype(BF16)
    fields[s] = jnp.dot(raw, select, preferred_element_type=F32).astype(BF16)
    nz_send[...] = noise_in[...].astype(F32).T.reshape(n_s, own, share).astype(BF16)
    nz_recv[s] = nz_send[s]

    pl.semaphore_wait(barrier, n_s + n_c - 2)

    def in_copies(j, slot, which=(0, 1, 2)):
        peer = src_peer(j)
        makers = [
            lambda: to_src(fields.at[slot], fields.at[slot], in_send.at[0, j], in_recv.at[0, j], peer),
            lambda: to_src(indices.at[slot], indices.at[slot], in_send.at[1, j], in_recv.at[1, j], peer),
            lambda: to_src(nz_send.at[peer], nz_recv.at[slot], in_send.at[2, j], in_recv.at[2, j], peer),
        ]
        return [makers[n]() for n in which]

    def start_inputs(j):
        for copy in in_copies(j, s):
            copy.start()

    each(n_s, start_inputs)

    dev_rows = s_dev + r_dev
    field_rows = n_s * dev_rows
    row = lax.broadcasted_iota(jnp.int32, (field_rows, 1), 0)
    group = jnp.zeros((field_rows, 1), jnp.int32)
    for k in range(1, n_s):
        group = group + jnp.where(row >= k * dev_rows, 1, 0)
    within = row - group * dev_rows
    is_source = within < s_dev
    source_id = jnp.where(is_source, group * s_dev + within, -1)
    receiver_id = jnp.where(is_source, -1, group * r_dev + within - s_dev)

    def wait_inputs(j):
        for copy in in_copies(j, src_peer(j), (0, 1)):
            copy.wait_recv()

    each(n_s, wait_inputs)

    for k in range(n_s):
        hit = (source_id == indices[k, 0] + k * s_dev) | (receiver_id == indices[k, 1])
        pick = jnp.where(hit, 1.0, 0.0).T.astype(BF16)
        for t in range(n_c):
            at = t * chunk + k * share
            picks[at : at + share, :] = pick[t * share : (t + 1) * share]
    every = fields[...].astype(F32).reshape(field_rows, cells)
    source_cols = jnp.where(is_source, every, 0.0).astype(BF16)
    receiver_cols = jnp.where(is_source, 0.0, every).astype(BF16)

    def build(k):
        at = pl.multiple_of(k * chunk, chunk)
        pick = picks[pl.ds(at, chunk), :]
        block = (
            jnp.dot(pick, source_cols, preferred_element_type=F32)
            * jnp.dot(pick, receiver_cols, preferred_element_type=F32)
        ).astype(BF16)
        oper[pl.ds(at, chunk), :] = block
        return block

    def rs_copy(phase, j, target):
        return to_cell(
            rs_send.at[phase, target], rs_recv.at[phase, j],
            rs_ssem.at[phase, j], rs_rsem.at[phase, j], target,
        )

    def forward(phase, low, after_sends):
        def part(k):
            at = pl.multiple_of(k * chunk, chunk)
            block = build(k) if phase == 0 else oper[pl.ds(at, chunk), :]
            return lax.dot_general(low, block, NT, preferred_element_type=F32)

        def one(j):
            target = cell_peer(j)
            rs_send[phase, target] = part(target).astype(BF16)
            rs_copy(phase, j, target).start()

        each(n_c, one)
        after_sends()
        rs_total = part(c)
        each(n_c, lambda j: rs_copy(phase, j, cell_peer(j)).wait_recv())
        for j in range(1, n_c):
            rs_total = rs_total + rs_recv[phase, j].astype(F32)
        return rs_total * scale

    def ag_copy(phase, j, slot):
        return to_cell(
            ag.at[phase, slot], ag.at[phase, slot],
            ag_ssem.at[phase, j], ag_rsem.at[phase, j], cell_peer(j),
        )

    def gather(phase, value):
        ag[phase, c] = value.astype(BF16)
        each(n_c, lambda j: ag_copy(phase, j, c).start())
        each(n_c, lambda j: ag_copy(phase, j, cell_peer(j)).wait_recv())
        return ag[phase].astype(F32)

    def stat_copy(step, j):
        return to_cell(
            stat_send.at[step], stat_recv.at[step, j],
            st_ssem.at[step, j], st_rsem.at[step, j], cell_peer(j),
        )

    diagonal = lax.broadcasted_iota(jnp.int32, (own, own), 0) == lax.broadcasted_iota(
        jnp.int32, (own, own), 1
    )

    def to_row(column):
        return jnp.sum(jnp.where(diagonal, column, 0.0), axis=0, keepdims=True)

    def to_column(row):
        return jnp.sum(jnp.where(diagonal, row, 0.0), axis=1, keepdims=True)

    def stat_start(step, first, second):
        top = lax.broadcasted_iota(jnp.int32, (8, own), 0) == 0
        stat_send[step] = jnp.where(top, to_row(first), to_row(second))
        each(n_c, lambda j: stat_copy(step, j).start())

    def stat_total(step):
        each(n_c, lambda j: stat_copy(step, j).wait_recv())
        total = stat_send[step]
        for j in range(1, n_c):
            total = total + stat_recv[step, j]
        return to_column(total[0:1]), to_column(total[1:2])

    own_models = models_in[...]
    first_data = forward(0, own_models, lambda: None)
    each(n_s, lambda j: in_copies(j, src_peer(j), (2,))[0].wait_recv())
    own_noise = jnp.concatenate([nz_recv[k].astype(F32) for k in range(n_s)], axis=1)
    chunk_res = -(first_data + own_noise)
    res[...] = gather(0, chunk_res)

    def pair_sum(values):
        return jnp.sum(jnp.sum(values, axis=0), axis=1, keepdims=True)

    for step in range(HSTEPS):
        last = step == HSTEPS - 1
        full = res[...]
        spread = pair_sum(full * full)
        delta = jnp.sqrt(spread / pairs_all + 1e-06)
        weight = delta[None] / jnp.maximum(jnp.abs(full), delta[None])
        weighted = weight * full
        for k in range(n_c):
            wlow[:, k * chunk : (k + 1) * chunk] = weighted[k].astype(BF16)
        grad = jnp.dot(wlow[...], oper[...], preferred_element_type=F32) * scale
        grads[step] = grad
        numer_own = jnp.sum(grad * grad, axis=1, keepdims=True)

        def send_numer():
            if not last:
                stat_start(step, numer_own, numer_own)

        image = forward(step + 1, grad.astype(BF16), send_numer)
        if last:
            own_full = chunk_res
            own_weight = delta / jnp.maximum(jnp.abs(own_full), delta)
            curve_own = jnp.sum(own_weight * image * image, axis=1, keepdims=True)
            stat_start(step, numer_own, curve_own)
            numer, curvature = stat_total(step)
            alpha = numer / (curvature + 1e-06)
        else:
            images = gather(step + 1, image)
            numer, _ = stat_total(step)
            curvature = pair_sum(weight * images * images)
            alpha = numer / (curvature + 1e-06)
            res[...] = full - alpha[None] * images
            grads[step] = alpha * grads[step]
        chunk_res = chunk_res - alpha * image

    for k in range(n_s):
        fin_send[k] = chunk_res[:, k * share : (k + 1) * share]

    def fin_copy(j, slot):
        return to_src(
            fin_send.at[src_peer(j)], fin_recv.at[slot], fin_ssem.at[j], fin_rsem.at[j], src_peer(j)
        )

    each(n_s, lambda j: fin_copy(j, s).start())
    fin_recv[s] = fin_send[s]
    total_rec = -(alpha * grads[HSTEPS - 1])
    for step in range(HSTEPS - 1):
        total_rec = total_rec - grads[step]
    rec_out[...] = total_rec

    def in_done(j):
        for copy in in_copies(j, s):
            copy.wait_send()

    each(n_s, in_done)
    for phase in range(HSTEPS + 1):
        each(n_c, lambda j, phase=phase: rs_copy(phase, j, cell_peer(j)).wait_send())
    for phase in range(HSTEPS):
        each(n_c, lambda j, phase=phase: ag_copy(phase, j, c).wait_send())
        each(n_c, lambda j, phase=phase: stat_copy(phase, j).wait_send())
    each(n_s, lambda j: fin_copy(j, src_peer(j)).wait_recv())
    res_out[...] = fin_recv[...].reshape(models_count, share).T
    each(n_s, lambda j: fin_copy(j, s).wait_send())


def shards(
    green_source, green_receiver, pair_source, pair_receiver, cell_order, test_models, data_noise
):
    n_s = lax.axis_size("src")
    n_c = lax.axis_size("cell")
    s_dev, cells = green_source.shape
    r_dev = green_receiver.shape[0]
    group_pairs = pair_source.shape[0]
    models_count = test_models.shape[0]
    own = models_count // n_s
    share = group_pairs // n_c
    chunk = share * n_s
    pairs_all = group_pairs * n_s
    dma = pltpu.SemaphoreType.DMA
    return pl.pallas_call(
        functools.partial(kernel_body, n_s, n_c),
        out_shape=(
            pltpu.VMEM((own, cells), F32),
            pltpu.VMEM((share, models_count), F32),
        ),
        in_specs=[pl.BlockSpec(memory_space=pltpu.HBM)] * 7,
        out_specs=[pl.BlockSpec(memory_space=pltpu.VMEM)] * 2,
        scratch_shapes=[
            pltpu.VMEM((s_dev, cells), BF16),
            pltpu.VMEM((r_dev, cells), BF16),
            pltpu.VMEM((1, cells), jnp.int32),
            pltpu.VMEM((own, cells), BF16),
            pltpu.VMEM((share, models_count), BF16),
            pltpu.VMEM((n_s, s_dev + r_dev, cells), BF16),
            pltpu.VMEM((n_s, 2, 1, group_pairs), jnp.int32),
            pltpu.VMEM((n_s, own, share), BF16),
            pltpu.VMEM((n_s, own, share), BF16),
            pltpu.VMEM((pairs_all, n_s * (s_dev + r_dev)), BF16),
            pltpu.VMEM((pairs_all, cells), BF16),
            pltpu.VMEM((HSTEPS + 1, n_c, own, chunk), BF16),
            pltpu.VMEM((HSTEPS + 1, n_c, own, chunk), BF16),
            pltpu.VMEM((HSTEPS, n_c, own, chunk), BF16),
            pltpu.VMEM((HSTEPS, 8, own), F32),
            pltpu.VMEM((HSTEPS, n_c, 8, own), F32),
            pltpu.VMEM((n_s, own, share), F32),
            pltpu.VMEM((n_s, own, share), F32),
            pltpu.VMEM((own, pairs_all), BF16),
            pltpu.VMEM((n_c, own, chunk), F32),
            pltpu.VMEM((HSTEPS, own, cells), F32),
            dma((7,)), dma((3, n_s)), dma((3, n_s)),
            dma((HSTEPS + 1, n_c)), dma((HSTEPS + 1, n_c)),
            dma((HSTEPS, n_c)), dma((HSTEPS, n_c)),
            dma((HSTEPS, n_c)), dma((HSTEPS, n_c)),
            dma((n_s,)), dma((n_s,)),
        ],
        compiler_params=pltpu.CompilerParams(
            collective_id=0, has_side_effects=True, vmem_limit_bytes=60 * 1024 * 1024
        ),
    )(
        green_source, green_receiver, pair_source[None, :], pair_receiver[None, :],
        cell_order, test_models, data_noise,
    )


def solution(mesh):
    return jax.shard_map(
        shards,
        mesh=mesh,
        in_specs=(
            P("src", "cell"),
            P("src", "cell"),
            P("src"),
            P("src"),
            P("cell", None),
            P(None, "cell"),
            P("src", None),
        ),
        out_specs=(P("src", "cell"), P(("src", "cell"), None)),
        check_vma=False,
    )
```

```python
import functools
import math

import jax
import jax.numpy as jnp
from jax import lax
from jax.experimental import pallas as pl
from jax.experimental.pallas import tpu as pltpu
from jax.sharding import PartitionSpec as P

HSTEPS = 2
MESH = pl.DeviceIdType.MESH
F32 = jnp.float32
BF16 = jnp.bfloat16
NT = (((1,), (1,)), ((), ()))


def each(count, body):
    if count <= 8:
        for i in range(count - 1, 0, -1):
            body(i)
    else:

        def step(i, carry):
            body(count - i)
            return carry

        lax.fori_loop(1, count, step, 0)


def kernel_body(
    n_s, n_c,
    gs, gr, ps, pr, order, models, noise,
    rec_out, res_out,
    gs_in, gr_in, order_in, models_in, noise_in,
    fields, indices, nz_send, nz_recv,
    picks, oper, rs_send, rs_recv, ag, stat_send, stat_recv,
    fin_send, fin_recv, wlow, res, grads,
    load, in_send, in_recv, rs_ssem, rs_rsem, ag_ssem, ag_rsem, st_ssem, st_rsem, fin_ssem, fin_rsem,
):
    s = lax.axis_index("src")
    c = lax.axis_index("cell")
    group_pairs = ps.shape[1]
    cells = gs.shape[1]
    models_count = models.shape[0]
    own = models_count // n_s
    share = group_pairs // n_c
    chunk = share * n_s
    pairs_all = group_pairs * n_s
    s_dev = gs.shape[0]
    r_dev = gr.shape[0]
    scale = 1.0 / math.sqrt(cells * n_c)

    def src_peer(j):
        return jnp.bitwise_xor(s, j)

    def cell_peer(j):
        return jnp.bitwise_xor(c, j)

    def to_src(src_ref, dst_ref, ssem, rsem, peer):
        return pltpu.make_async_remote_copy(
            src_ref=src_ref, dst_ref=dst_ref, send_sem=ssem, recv_sem=rsem,
            device_id={"src": peer}, device_id_type=MESH,
        )

    def to_cell(src_ref, dst_ref, ssem, rsem, peer):
        return pltpu.make_async_remote_copy(
            src_ref=src_ref, dst_ref=dst_ref, send_sem=ssem, recv_sem=rsem,
            device_id={"cell": peer}, device_id_type=MESH,
        )

    barrier = pltpu.get_barrier_semaphore()
    each(n_s, lambda j: pl.semaphore_signal(
        barrier, inc=1, device_id={"src": src_peer(j)}, device_id_type=MESH))
    each(n_c, lambda j: pl.semaphore_signal(
        barrier, inc=1, device_id={"cell": cell_peer(j)}, device_id_type=MESH))

    loads = [
        pltpu.make_async_copy(order, order_in, load.at[0]),
        pltpu.make_async_copy(gs, gs_in, load.at[1]),
        pltpu.make_async_copy(gr, gr_in, load.at[2]),
        pltpu.make_async_copy(ps, indices.at[s, 0], load.at[3]),
        pltpu.make_async_copy(pr, indices.at[s, 1], load.at[4]),
        pltpu.make_async_copy(
            noise.at[pl.ds(pl.multiple_of(c * share, share), share), :], noise_in, load.at[5]),
        pltpu.make_async_copy(
            models.at[pl.ds(pl.multiple_of(s * own, own), own), :], models_in, load.at[6]),
    ]
    for copy in loads:
        copy.start()
    for copy in loads:
        copy.wait()
    rows = lax.broadcasted_iota(jnp.int32, (cells, cells), 0)
    select = jnp.where(rows == order_in[...], 1.0, 0.0).astype(BF16)
    raw = jnp.concatenate([gs_in[...].astype(F32), gr_in[...].astype(F32)], axis=0).astype(BF16)
    fields[s] = jnp.dot(raw, select, preferred_element_type=F32).astype(BF16)
    nz_send[...] = noise_in[...].astype(F32).T.reshape(n_s, own, share).astype(BF16)
    nz_recv[s] = nz_send[s]

    pl.semaphore_wait(barrier, n_s + n_c - 2)

    def in_copies(j, slot, which=(0, 1, 2)):
        peer = src_peer(j)
        makers = [
            lambda: to_src(fields.at[slot], fields.at[slot], in_send.at[0, j], in_recv.at[0, j], peer),
            lambda: to_src(indices.at[slot], indices.at[slot], in_send.at[1, j], in_recv.at[1, j], peer),
            lambda: to_src(nz_send.at[peer], nz_recv.at[slot], in_send.at[2, j], in_recv.at[2, j], peer),
        ]
        return [makers[n]() for n in which]

    each(n_s, lambda j: in_copies(j, s, (1,))[0].start())
    each(n_s, lambda j: in_copies(j, s, (0,))[0].start())
    each(n_s, lambda j: in_copies(j, s, (2,))[0].start())

    dev_rows = s_dev + r_dev
    field_rows = n_s * dev_rows
    row = lax.broadcasted_iota(jnp.int32, (field_rows, 1), 0)
    group = jnp.zeros((field_rows, 1), jnp.int32)
    for k in range(1, n_s):
        group = group + jnp.where(row >= k * dev_rows, 1, 0)
    within = row - group * dev_rows
    is_source = within < s_dev
    source_id = jnp.where(is_source, group * s_dev + within, -1)
    receiver_id = jnp.where(is_source, -1, group * r_dev + within - s_dev)

    each(n_s, lambda j: in_copies(j, src_peer(j), (1,))[0].wait_recv())

    for k in range(n_s):
        hit = (source_id == indices[k, 0] + k * s_dev) | (receiver_id == indices[k, 1])
        pick = jnp.where(hit, 1.0, 0.0).T.astype(BF16)
        for t in range(n_c):
            at = t * chunk + k * share
            picks[at : at + share, :] = pick[t * share : (t + 1) * share]
    each(n_s, lambda j: in_copies(j, src_peer(j), (0,))[0].wait_recv())
    every = fields[...].astype(F32).reshape(field_rows, cells)
    source_cols = jnp.where(is_source, every, 0.0).astype(BF16)
    receiver_cols = jnp.where(is_source, 0.0, every).astype(BF16)

    def build(k):
        at = pl.multiple_of(k * chunk, chunk)
        pick = picks[pl.ds(at, chunk), :]
        block = (
            jnp.dot(pick, source_cols, preferred_element_type=F32)
            * jnp.dot(pick, receiver_cols, preferred_element_type=F32)
        ).astype(BF16)
        oper[pl.ds(at, chunk), :] = block
        return block

    def rs_copy(phase, j, target):
        return to_cell(
            rs_send.at[phase, target], rs_recv.at[phase, j],
            rs_ssem.at[phase, j], rs_rsem.at[phase, j], target,
        )

    def forward(phase, low, after_sends):
        def part(k):
            at = pl.multiple_of(k * chunk, chunk)
            block = build(k) if phase == 0 else oper[pl.ds(at, chunk), :]
            return lax.dot_general(low, block, NT, preferred_element_type=F32)

        def one(j):
            target = cell_peer(j)
            rs_send[phase, target] = part(target).astype(BF16)
            rs_copy(phase, j, target).start()

        each(n_c, one)
        after_sends()
        rs_total = part(c)
        each(n_c, lambda j: rs_copy(phase, j, cell_peer(j)).wait_recv())
        for j in range(1, n_c):
            rs_total = rs_total + rs_recv[phase, j].astype(F32)
        return rs_total * scale

    def ag_copy(phase, j, slot):
        return to_cell(
            ag.at[phase, slot], ag.at[phase, slot],
            ag_ssem.at[phase, j], ag_rsem.at[phase, j], cell_peer(j),
        )

    def gather(phase, value):
        ag[phase, c] = value.astype(BF16)
        each(n_c, lambda j: ag_copy(phase, j, c).start())
        each(n_c, lambda j: ag_copy(phase, j, cell_peer(j)).wait_recv())
        return ag[phase].astype(F32)

    def stat_copy(step, j):
        return to_cell(
            stat_send.at[step], stat_recv.at[step, j],
            st_ssem.at[step, j], st_rsem.at[step, j], cell_peer(j),
        )

    diagonal = lax.broadcasted_iota(jnp.int32, (own, own), 0) == lax.broadcasted_iota(
        jnp.int32, (own, own), 1
    )

    def to_row(column):
        return jnp.sum(jnp.where(diagonal, column, 0.0), axis=0, keepdims=True)

    def to_column(row):
        return jnp.sum(jnp.where(diagonal, row, 0.0), axis=1, keepdims=True)

    def stat_start(step, first, second):
        top = lax.broadcasted_iota(jnp.int32, (8, own), 0) == 0
        stat_send[step] = jnp.where(top, to_row(first), to_row(second))
        each(n_c, lambda j: stat_copy(step, j).start())

    def stat_total(step):
        each(n_c, lambda j: stat_copy(step, j).wait_recv())
        total = stat_send[step]
        for j in range(1, n_c):
            total = total + stat_recv[step, j]
        return to_column(total[0:1]), to_column(total[1:2])

    own_models = models_in[...]
    first_data = forward(0, own_models, lambda: None)
    each(n_s, lambda j: in_copies(j, src_peer(j), (2,))[0].wait_recv())
    own_noise = jnp.concatenate([nz_recv[k].astype(F32) for k in range(n_s)], axis=1)
    chunk_res = -(first_data + own_noise)
    res[...] = gather(0, chunk_res)

    def pair_sum(values):
        return jnp.sum(jnp.sum(values, axis=0), axis=1, keepdims=True)

    alphas = []
    for step in range(HSTEPS):
        last = step == HSTEPS - 1
        full = res[...]
        spread = pair_sum(full * full)
        delta = jnp.sqrt(spread / pairs_all + 1e-06)
        weight = delta[None] / jnp.maximum(jnp.abs(full), delta[None])
        weighted = weight * full
        for k in range(n_c):
            wlow[:, k * chunk : (k + 1) * chunk] = weighted[k].astype(BF16)
        grad = jnp.dot(wlow[...], oper[...], preferred_element_type=F32) * scale
        after = []

        def send_numer():
            grads[step] = grad
            numer_own = jnp.sum(grad * grad, axis=1, keepdims=True)
            after.append(numer_own)
            if last:
                after.append(delta / jnp.maximum(jnp.abs(chunk_res), delta))
            else:
                stat_start(step, numer_own, numer_own)

        image = forward(step + 1, grad.astype(BF16), send_numer)
        if last:
            curve_own = jnp.sum(after[1] * image * image, axis=1, keepdims=True)
            stat_start(step, after[0], curve_own)
            numer, curvature = stat_total(step)
            alpha = numer / (curvature + 1e-06)
        else:
            images = gather(step + 1, image)
            numer, _ = stat_total(step)
            curvature = pair_sum(weight * images * images)
            alpha = numer / (curvature + 1e-06)
            res[...] = full - alpha[None] * images
        chunk_res = chunk_res - alpha * image
        alphas.append(alpha)

    for k in range(n_s):
        fin_send[k] = chunk_res[:, k * share : (k + 1) * share]

    def fin_copy(j, slot):
        return to_src(
            fin_send.at[src_peer(j)], fin_recv.at[slot], fin_ssem.at[j], fin_rsem.at[j], src_peer(j)
        )

    each(n_s, lambda j: fin_copy(j, s).start())
    fin_recv[s] = fin_send[s]
    total_rec = -(alphas[0] * grads[0])
    for step in range(1, HSTEPS):
        total_rec = total_rec - alphas[step] * grads[step]
    rec_out[...] = total_rec

    def in_done(j):
        for copy in in_copies(j, s):
            copy.wait_send()

    each(n_s, in_done)
    for phase in range(HSTEPS + 1):
        each(n_c, lambda j, phase=phase: rs_copy(phase, j, cell_peer(j)).wait_send())
    for phase in range(HSTEPS):
        each(n_c, lambda j, phase=phase: ag_copy(phase, j, c).wait_send())
        each(n_c, lambda j, phase=phase: stat_copy(phase, j).wait_send())
    each(n_s, lambda j: fin_copy(j, src_peer(j)).wait_recv())
    res_out[...] = fin_recv[...].reshape(models_count, share).T
    each(n_s, lambda j: fin_copy(j, s).wait_send())


def shards(
    green_source, green_receiver, pair_source, pair_receiver, cell_order, test_models, data_noise
):
    n_s = lax.axis_size("src")
    n_c = lax.axis_size("cell")
    s_dev, cells = green_source.shape
    r_dev = green_receiver.shape[0]
    group_pairs = pair_source.shape[0]
    models_count = test_models.shape[0]
    own = models_count // n_s
    share = group_pairs // n_c
    chunk = share * n_s
    pairs_all = group_pairs * n_s
    dma = pltpu.SemaphoreType.DMA
    return pl.pallas_call(
        functools.partial(kernel_body, n_s, n_c),
        out_shape=(
            pltpu.VMEM((own, cells), F32),
            pltpu.VMEM((share, models_count), F32),
        ),
        in_specs=[pl.BlockSpec(memory_space=pltpu.HBM)] * 7,
        out_specs=[pl.BlockSpec(memory_space=pltpu.VMEM)] * 2,
        scratch_shapes=[
            pltpu.VMEM((s_dev, cells), BF16),
            pltpu.VMEM((r_dev, cells), BF16),
            pltpu.VMEM((1, cells), jnp.int32),
            pltpu.VMEM((own, cells), BF16),
            pltpu.VMEM((share, models_count), BF16),
            pltpu.VMEM((n_s, s_dev + r_dev, cells), BF16),
            pltpu.VMEM((n_s, 2, 1, group_pairs), jnp.int32),
            pltpu.VMEM((n_s, own, share), BF16),
            pltpu.VMEM((n_s, own, share), BF16),
            pltpu.VMEM((pairs_all, n_s * (s_dev + r_dev)), BF16),
            pltpu.VMEM((pairs_all, cells), BF16),
            pltpu.VMEM((HSTEPS + 1, n_c, own, chunk), BF16),
            pltpu.VMEM((HSTEPS + 1, n_c, own, chunk), BF16),
            pltpu.VMEM((HSTEPS, n_c, own, chunk), BF16),
            pltpu.VMEM((HSTEPS, 8, own), F32),
            pltpu.VMEM((HSTEPS, n_c, 8, own), F32),
            pltpu.VMEM((n_s, own, share), F32),
            pltpu.VMEM((n_s, own, share), F32),
            pltpu.VMEM((own, pairs_all), BF16),
            pltpu.VMEM((n_c, own, chunk), F32),
            pltpu.VMEM((HSTEPS, own, cells), F32),
            dma((7,)), dma((3, n_s)), dma((3, n_s)),
            dma((HSTEPS + 1, n_c)), dma((HSTEPS + 1, n_c)),
            dma((HSTEPS, n_c)), dma((HSTEPS, n_c)),
            dma((HSTEPS, n_c)), dma((HSTEPS, n_c)),
            dma((n_s,)), dma((n_s,)),
        ],
        compiler_params=pltpu.CompilerParams(
            collective_id=0, has_side_effects=True, vmem_limit_bytes=60 * 1024 * 1024
        ),
    )(
        green_source, green_receiver, pair_source[None, :], pair_receiver[None, :],
        cell_order, test_models, data_noise,
    )


def solution(mesh):
    return jax.shard_map(
        shards,
        mesh=mesh,
        in_specs=(
            P("src", "cell"),
            P("src", "cell"),
            P("src"),
            P("src"),
            P("cell", None),
            P(None, "cell"),
            P("src", None),
        ),
        out_specs=(P("src", "cell"), P(("src", "cell"), None)),
        check_vma=False,
    )
```
